32 devices in a mesh: row: 4 (over z), col: 8 (over y, x, core).
Axes of the slice: x: 2, y: 2, z: 4, core: 2. Of those that a mesh axis runs over, the one named last changes fastest.
Arguments:
- factor_panel: bfloat16 [2, 1536, 24576], P(None, 'row', 'col'), may hold values from -0.0390625 to 0.0390625
- solved_trail: bfloat16 [24576, 384], P('col'), may hold values from -6 to 6
- right_sides: bfloat16 [2, 1536, 384], P(None, 'row'), may hold values from -6 to 6
- diag_inverse: bfloat16 [2, 1536, 1536], P(None, 'row'), may hold values from -1 to 1.5, as said below
- coupling: bfloat16 [1536, 1536], P('row'), may hold values from -0.15625 to 0.15625
Outputs:
- solution: bfloat16 [2, 1536, 384], P(None, 'row')
The draws below stay inside these ranges and needn't reach their ends.
Inputs may be any that keep to these rules, and one draw needn't show every extreme that they name: Each diag_inverse[b] is upper triangular with a diagonal between 0.6 and 1.4.
All inputs are finite; a program needn't handle non-finite values.
Results may differ from the reference program's by a relative error of at most 0.0057.
Values may be sent and summed in bfloat16 or wider, within the bound.
A program may use at most 64 MiB of HBM per device.

```python
import math
import jax
import jax.numpy as jnp

TILE = 1536
FRAMES = 384
TRAIL_ROWS = 24576


def draw_diag_inverse(key, part):
    key_diag, key_off = jax.random.split(jax.random.fold_in(key, 17))
    diagonal = jax.random.uniform(key_diag, (2, TILE), jnp.float32, 0.6, 1.4)
    offdiag = jnp.clip(jax.random.normal(key_off, (2, TILE, TILE), jnp.float32), -4.0, 4.0)
    offdiag = offdiag * (0.8 / math.sqrt(TILE))
    rowidx = jnp.arange(TILE)[:, None]
    colidx = jnp.arange(TILE)[None, :]
    upper = jnp.where(colidx > rowidx, offdiag, 0.0)
    eyemat = (rowidx == colidx).astype(jnp.float32)
    return (upper + eyemat[None, :, :] * diagonal[:, :, None]).astype(jnp.bfloat16)


def level_of(key, dims, cuts, least, largest):
    def one(position, shards_of):
        draws = jax.random.uniform(jax.random.fold_in(jax.random.fold_in(key, 6), position), (shards_of,), jnp.float32, least / len(cuts), largest / len(cuts))
        return jnp.repeat(jnp.exp(draws), dims[position] // shards_of).reshape((-1,) + (1,) * (len(dims) - position - 1))

    factor_of = one(*cuts[0])
    for cut in cuts[1:]:
        factor_of = factor_of * one(*cut)
    return factor_of


def bell_draw(own_key, extent, spread, limit, cuts=(), dtype=jnp.bfloat16):
    entries = spread * jax.random.normal(own_key, extent, jnp.float32)
    if cuts:
        entries = entries * level_of(own_key, extent, cuts, -0.22, 0.18)
    return jnp.clip(entries, -limit, limit).astype(dtype)


def setup_inputs(seed: int = 0) -> dict:
    splits = jax.random.split(jax.random.key(seed), 6)
    factor_panel = bell_draw(splits[0], (2, TILE, TRAIL_ROWS), TRAIL_ROWS ** -0.5, 0.0390625, ((1, 4), (2, 8)))
    solved_trail = bell_draw(splits[1], (TRAIL_ROWS, FRAMES), 1.0, 6.0, ((0, 8),))
    right_sides = bell_draw(splits[2], (2, TILE, FRAMES), 1.0, 6.0, ((1, 4),))
    diag_inverse = draw_diag_inverse(jax.random.fold_in(splits[5], 71), 0)
    coupling = bell_draw(splits[4], (TILE, TILE), TILE ** -0.5, 0.15625, ((0, 4),))
    return {"factor_panel": factor_panel, "solved_trail": solved_trail, "right_sides": right_sides, "diag_inverse": diag_inverse, "coupling": coupling}


def reference(factor_panel, solved_trail, right_sides, diag_inverse, coupling):
    lower_tot = jnp.dot(factor_panel[1], solved_trail, preferred_element_type=jnp.float32)
    upper_tot = jnp.dot(factor_panel[0], solved_trail, preferred_element_type=jnp.float32)
    next_res = (right_sides[1].astype(jnp.float32) - lower_tot).astype(jnp.bfloat16)
    next_sol = jnp.dot(diag_inverse[1], next_res, preferred_element_type=jnp.float32).astype(jnp.bfloat16)
    carried = jnp.dot(coupling, next_sol, preferred_element_type=jnp.float32)
    first_res = (right_sides[0].astype(jnp.float32) - upper_tot - carried).astype(jnp.bfloat16)
    first_sol = jnp.dot(diag_inverse[0], first_res, preferred_element_type=jnp.float32).astype(jnp.bfloat16)
    return jnp.stack([first_sol, next_sol])
```

```python
import functools

import jax
import jax.numpy as jnp
from jax import lax
from jax.experimental import pallas as pl
from jax.experimental.pallas import tpu as pltpu
from jax.sharding import PartitionSpec as P

F32 = jnp.float32
BF16 = jnp.bfloat16
MESH = pl.DeviceIdType.MESH


def substitute(totals, rights, diag_inverse, coupling):
    next_res = (rights[1].astype(F32) - totals[1]).astype(BF16)
    next_all = lax.all_gather(next_res, "row", axis=0, tiled=True)
    next_sol = jnp.dot(diag_inverse[1], next_all, preferred_element_type=F32).astype(BF16)
    sol_all = lax.all_gather(next_sol, "row", axis=0, tiled=True)
    carried = jnp.dot(coupling, sol_all, preferred_element_type=F32)
    first_res = (rights[0].astype(F32) - totals[0] - carried).astype(BF16)
    first_all = lax.all_gather(first_res, "row", axis=0, tiled=True)
    first_sol = jnp.dot(diag_inverse[0], first_all, preferred_element_type=F32).astype(BF16)
    return jnp.stack([first_sol, next_sol])


def plain_shards(factor_panel, solved_trail, right_sides, diag_inverse, coupling):
    partial_value = jnp.einsum(
        "bik,kf->bif", factor_panel, solved_trail, preferred_element_type=F32
    )
    totals = lax.psum(partial_value, "col")
    return substitute(totals, right_sides, diag_inverse, coupling)


def dot_t(a, b):
    return lax.dot_general(a, b, (((1,), (1,)), ((), ())), preferred_element_type=F32)


def kernel(
    R, C, nk,
    panel, trail, right, diag, coup, out,
    pbuf, tbuf, hbuf, mbuf, acc, acc_t, h_t, sbuf, gbuf, zbuf, zacc, fbuf,
    psem, tsem, hsem, msem, lsem, gsend, grecv, zsend, zrecv, fsend, frecv,
):
    r = lax.axis_index("row")
    c = lax.axis_index("col")
    m, frames = hbuf.shape[1], hbuf.shape[2]
    kc = tbuf.shape[1]
    fs = frames // C

    def flip(d):
        total = 0
        bit = 1
        while bit < C:
            mine = (c // bit) % 2
            total = total + (((mine + 1) % 2) if d & bit else mine) * bit
            bit *= 2
        return total

    peers = [flip(d) for d in range(1, C)][::-1]

    def panel_copy(b, i):
        return pltpu.make_async_copy(
            panel.at[b, :, pl.ds(i * kc, kc)], pbuf.at[b, i], psem.at[b, i]
        )

    def trail_copy(i):
        return pltpu.make_async_copy(trail.at[pl.ds(i * kc, kc), :], tbuf.at[i], tsem.at[i])

    def mat_copy(b, j):
        src = coup.at[:, pl.ds(j * m, m)] if b == 2 else diag.at[b, :, pl.ds(j * m, m)]
        return pltpu.make_async_copy(src, mbuf.at[b, j], msem.at[b, j])

    right_copy = pltpu.make_async_copy(right, hbuf, hsem)
    for i in range(nk):
        trail_copy(i).start()
        panel_copy(1, i).start()
    for i in range(nk):
        panel_copy(0, i).start()
    right_copy.start()
    for b in (1, 2, 0):
        for j in range(R):
            mat_copy(b, j).start()

    barrier = pltpu.get_barrier_semaphore()
    for p in peers:
        pl.semaphore_signal(barrier, inc=1, device_id=(r, p), device_id_type=MESH)
    for d in range(1, R):
        pl.semaphore_signal(
            barrier, inc=1, device_id=(lax.rem(r + d, R), c), device_id_type=MESH
        )

    def part_send(b, n):
        p = peers[n]
        return pltpu.make_async_remote_copy(
            src_ref=sbuf.at[b, p], dst_ref=gbuf.at[b, c],
            send_sem=gsend.at[b, n], recv_sem=grecv.at[b, c],
            device_id=(r, p), device_id_type=MESH,
        )

    def part_recv(b, n):
        p = peers[n]
        return pltpu.make_async_remote_copy(
            src_ref=sbuf.at[b, p], dst_ref=gbuf.at[b, p],
            send_sem=gsend.at[b, n], recv_sem=grecv.at[b, p],
            device_id=(r, p), device_id_type=MESH,
        )

    def partials(b):
        for i in range(nk):
            if b == 1:
                trail_copy(i).wait()
            panel_copy(b, i).wait()
            term = jnp.dot(pbuf[b, i], tbuf[i], preferred_element_type=F32)
            if i == 0:
                acc[...] = term
            else:
                acc[...] += term
        turned = acc[...].T.reshape(C, fs, m)
        sbuf[b] = turned.astype(BF16)
        acc_t[b] = turned

    partials(1)
    pl.semaphore_wait(barrier, C - 1 + R - 1)
    for n in range(C - 1):
        part_send(1, n).start()
    partials(0)
    for n in range(C - 1):
        part_send(0, n).start()
    right_copy.wait()
    for b in (1, 0):
        h_t[b] = hbuf[b].astype(F32).T.reshape(C, fs, m)
    for b in (1, 2, 0):
        for j in range(R):
            mat_copy(b, j).wait()

    def residual(b):
        total = acc_t[b, c]
        for n in reversed(range(C - 1)):
            part_recv(b, n).wait_recv()
            total = total + gbuf[b, peers[n]].astype(F32)
        return h_t[b, c] - total

    def row_send(phase, j):
        return pltpu.make_async_remote_copy(
            src_ref=zbuf.at[phase, r], dst_ref=zbuf.at[phase, r],
            send_sem=zsend.at[phase, j], recv_sem=zrecv.at[phase, r],
            device_id=(j, c), device_id_type=MESH,
        )

    def row_recv(phase, j):
        return pltpu.make_async_remote_copy(
            src_ref=zbuf.at[phase, j], dst_ref=zbuf.at[phase, j],
            send_sem=zsend.at[phase, j], recv_sem=zrecv.at[phase, j],
            device_id=(j, c), device_id_type=MESH,
        )

    def triangle(phase, b, value):
        zbuf[phase, r] = value
        for d in reversed(range(1, R)):
            @pl.when(r - d >= 0)
            def _():
                row_send(phase, r - d).start()
        zacc[...] = dot_t(zbuf[phase, r], mbuf[b, r])
        for d in range(1, R):
            @pl.when(r + d < R)
            def _():
                row_recv(phase, r + d).wait_recv()
                zacc[...] += dot_t(zbuf[phase, r + d], mbuf[b, r + d])
        return zacc[...].astype(BF16)

    def sol_send(b, n):
        p = peers[n]
        return pltpu.make_async_remote_copy(
            src_ref=fbuf.at[b], dst_ref=out.at[b, c],
            send_sem=fsend.at[b, n], recv_sem=frecv.at[b, c],
            device_id=(r, p), device_id_type=MESH,
        )

    def sol_recv(b, n):
        p = peers[n]
        return pltpu.make_async_remote_copy(
            src_ref=fbuf.at[b], dst_ref=out.at[b, p],
            send_sem=fsend.at[b, n], recv_sem=frecv.at[b, p],
            device_id=(r, p), device_id_type=MESH,
        )

    def own_copy(b):
        return pltpu.make_async_copy(fbuf.at[b], out.at[b, c], lsem.at[b])

    next_sol = triangle(0, 1, residual(1).astype(BF16))

    zbuf[1, r] = next_sol
    for d in reversed(range(1, R)):
        @pl.when(r - d >= 0)
        def _():
            row_send(1, r - d).start()

        @pl.when(r + d < R)
        def _():
            row_send(1, r + d).start()
    fbuf[1] = next_sol
    for n in range(C - 1):
        sol_send(1, n).start()
    own_copy(1).start()

    zacc[...] = residual(0)
    for j in reversed(range(R)):
        @pl.when(r != j)
        def _():
            row_recv(1, j).wait_recv()
        zacc[...] -= dot_t(zbuf[1, j], mbuf[2, j])

    first_sol = triangle(2, 0, zacc[...].astype(BF16))
    fbuf[0] = first_sol
    for n in range(C - 1):
        sol_send(0, n).start()
    own_copy(0).start()

    for b in (1, 0):
        own_copy(b).wait()
        for n in range(C - 1):
            sol_recv(b, n).wait_recv()
    for b in (1, 0):
        for n in range(C - 1):
            part_send(b, n).wait_send()
            sol_send(b, n).wait_send()
    for phase in range(3):
        for d in range(1, R):
            @pl.when(r - d >= 0)
            def _():
                row_send(phase, r - d).wait_send()
            if phase == 1:
                @pl.when(r + d < R)
                def _():
                    row_send(phase, r + d).wait_send()


def fused_shards(R, C, factor_panel, solved_trail, right_sides, diag_inverse, coupling):
    _, m, k = factor_panel.shape
    frames = solved_trail.shape[1]
    fs = frames // C
    nk = 4
    kc = k // nk
    any_spec = pl.BlockSpec(memory_space=pl.ANY)
    DMA = pltpu.SemaphoreType.DMA
    out = pl.pallas_call(
        functools.partial(kernel, R, C, nk),
        out_shape=jax.ShapeDtypeStruct((2, C, fs, m), BF16),
        in_specs=[any_spec] * 5,
        out_specs=any_spec,
        scratch_shapes=[
            pltpu.VMEM((2, nk, m, kc), BF16),
            pltpu.VMEM((nk, kc, frames), BF16),
            pltpu.VMEM((2, m, frames), BF16),
            pltpu.VMEM((3, R, m, m), BF16),
            pltpu.VMEM((m, frames), F32),
            pltpu.VMEM((2, C, fs, m), F32),
            pltpu.VMEM((2, C, fs, m), F32),
            pltpu.VMEM((2, C, fs, m), BF16),
            pltpu.VMEM((2, C, fs, m), BF16),
            pltpu.VMEM((3, R, fs, m), BF16),
            pltpu.VMEM((fs, m), F32),
            pltpu.VMEM((2, fs, m), BF16),
            DMA((2, nk)),
            DMA((nk,)),
            DMA,
            DMA((3, R)),
            DMA((2,)),
            DMA((2, C - 1)),
            DMA((2, C)),
            DMA((3, R)),
            DMA((3, R)),
            DMA((2, C - 1)),
            DMA((2, C)),
        ],
        compiler_params=pltpu.CompilerParams(collective_id=0, has_side_effects=True),
    )(factor_panel, solved_trail, right_sides, diag_inverse, coupling)
    return jnp.swapaxes(out.reshape(2, frames, m), 1, 2)


def solution(mesh):
    R, C = mesh.shape["row"], mesh.shape["col"]

    def shards(factor_panel, solved_trail, right_sides, diag_inverse, coupling):
        _, m, k = factor_panel.shape
        frames = solved_trail.shape[1]
        fits = (
            C & (C - 1) == 0 and frames % (16 * C) == 0 and m % 128 == 0
            and frames % 128 == 0 and k % 512 == 0
        )
        args = (factor_panel, solved_trail, right_sides, diag_inverse, coupling)
        return fused_shards(R, C, *args) if fits else plain_shards(*args)

    in_specs = (
        P(None, "row", "col"),
        P("col", None),
        P(None, "row", None),
        P(None, "row", None),
        P("row", None),
    )
    out_specs = P(None, "row", None)
    return jax.shard_map(shards, mesh=mesh, in_specs=in_specs, out_specs=out_specs, check_vma=False)
```

```python
import functools

import jax
import jax.numpy as jnp
from jax import lax
from jax.experimental import pallas as pl
from jax.experimental.pallas import tpu as pltpu
from jax.sharding import PartitionSpec as P

F32 = jnp.float32
BF16 = jnp.bfloat16
MESH = pl.DeviceIdType.MESH


def substitute(totals, rights, diag_inverse, coupling):
    next_res = (rights[1].astype(F32) - totals[1]).astype(BF16)
    next_all = lax.all_gather(next_res, "row", axis=0, tiled=True)
    next_sol = jnp.dot(diag_inverse[1], next_all, preferred_element_type=F32).astype(BF16)
    sol_all = lax.all_gather(next_sol, "row", axis=0, tiled=True)
    carried = jnp.dot(coupling, sol_all, preferred_element_type=F32)
    first_res = (rights[0].astype(F32) - totals[0] - carried).astype(BF16)
    first_all = lax.all_gather(first_res, "row", axis=0, tiled=True)
    first_sol = jnp.dot(diag_inverse[0], first_all, preferred_element_type=F32).astype(BF16)
    return jnp.stack([first_sol, next_sol])


def plain_shards(factor_panel, solved_trail, right_sides, diag_inverse, coupling):
    partial_value = jnp.einsum(
        "bik,kf->bif", factor_panel, solved_trail, preferred_element_type=F32
    )
    totals = lax.psum(partial_value, "col")
    return substitute(totals, right_sides, diag_inverse, coupling)


def dot_t(a, b):
    return lax.dot_general(a, b, (((1,), (1,)), ((), ())), preferred_element_type=F32)


def kernel(
    R, C, nk,
    panel, trail, right, diag, coup, out,
    pbuf, tbuf, hbuf, mbuf, acc, acc_t, h_t, sbuf, gbuf, zbuf, zacc, fbuf, xbuf, ybuf,
    psem, tsem, hsem, msem, lsem, gsend, grecv, zsend, zrecv, fsend, frecv, xsend, xrecv,
):
    r = lax.axis_index("row")
    c = lax.axis_index("col")
    m, frames = hbuf.shape[1], hbuf.shape[2]
    kc = tbuf.shape[1]
    fs = frames // C

    def flip(d):
        total = 0
        bit = 1
        while bit < C:
            mine = (c // bit) % 2
            total = total + (((mine + 1) % 2) if d & bit else mine) * bit
            bit *= 2
        return total

    peers = [flip(d) for d in range(1, C)][::-1]
    H = C // 2
    def slot(p):
        return (p % 2) * H + p // 2
    core, mate = c % 2, flip(1)
    chips = [flip(d) for d in range(2, C, 2)][::-1]
    me = slot(c)

    def panel_copy(b, i):
        return pltpu.make_async_copy(
            panel.at[b, :, pl.ds(i * kc, kc)], pbuf.at[b, i], psem.at[b, i]
        )

    def trail_copy(i):
        return pltpu.make_async_copy(trail.at[pl.ds(i * kc, kc), :], tbuf.at[i], tsem.at[i])

    def mat_copy(b, j):
        src = coup.at[:, pl.ds(j * m, m)] if b == 2 else diag.at[b, :, pl.ds(j * m, m)]
        return pltpu.make_async_copy(src, mbuf.at[b, j], msem.at[b, j])

    right_copy = pltpu.make_async_copy(right, hbuf, hsem)
    for i in range(nk):
        trail_copy(i).start()
        panel_copy(1, i).start()
    def late0():
        for i in range(nk):
            panel_copy(0, i).start()
        right_copy.start()

    def late1():
        for b in (1, 2, 0):
            for j in range(R):
                mat_copy(b, j).start()


    barrier = pltpu.get_barrier_semaphore()
    for p in peers:
        pl.semaphore_signal(barrier, inc=1, device_id=(r, p), device_id_type=MESH)
    for d in range(1, R):
        pl.semaphore_signal(
            barrier, inc=1, device_id=(lax.rem(r + d, R), c), device_id_type=MESH
        )

    def partials(b):
        for i in range(nk):
            if b == 1:
                trail_copy(i).wait()
            panel_copy(b, i).wait()
            term = jnp.dot(pbuf[b, i], tbuf[i], preferred_element_type=F32)
            if i == 0:
                acc[...] = term
            else:
                acc[...] += term
        turned = acc[...].T.reshape(C, fs, m)
        sbuf[b] = turned.astype(BF16)
        acc_t[b] = turned


    def x_copy(b):
        return pltpu.make_async_remote_copy(
            src_ref=sbuf.at[b, pl.ds((1 - core) * H, H)], dst_ref=xbuf.at[b],
            send_sem=xsend.at[b], recv_sem=xrecv.at[b],
            device_id=(r, mate), device_id_type=MESH,
        )

    def y_copy(b, n, dst):
        p = chips[n]
        return pltpu.make_async_remote_copy(
            src_ref=ybuf.at[b, p // 2], dst_ref=gbuf.at[b, dst],
            send_sem=gsend.at[b, n], recv_sem=grecv.at[b, dst],
            device_id=(r, p), device_id_type=MESH,
        )

    def mid(b):
        x_copy(b).wait_recv()
        both = acc_t[b, pl.ds(core * H, H)] + xbuf[b].astype(F32)
        acc_t[b, pl.ds(core * H, H)] = both
        ybuf[b] = both.astype(BF16)
        for n in range(H - 1):
            y_copy(b, n, c).start()

    def first_send(b):
        x_copy(b).start()

    partials(1)
    late0()
    pl.semaphore_wait(barrier, C - 1 + R - 1)
    first_send(1)
    mid(1)
    partials(0)
    late1()
    first_send(0)
    right_copy.wait()
    for b in (1, 0):
        h_t[b] = hbuf[b].astype(F32).T.reshape(C, fs, m)
    mid(0)
    for b in (1, 2, 0):
        for j in range(R):
            mat_copy(b, j).wait()

    def residual(b):
        total = acc_t[b, me]
        for n in reversed(range(H - 1)):
            y_copy(b, n, chips[n]).wait_recv()
            total = total + gbuf[b, chips[n]].astype(F32)
        return h_t[b, me] - total

    def row_send(phase, j):
        return pltpu.make_async_remote_copy(
            src_ref=zbuf.at[phase, r], dst_ref=zbuf.at[phase, r],
            send_sem=zsend.at[phase, j], recv_sem=zrecv.at[phase, r],
            device_id=(j, c), device_id_type=MESH,
        )

    def row_recv(phase, j):
        return pltpu.make_async_remote_copy(
            src_ref=zbuf.at[phase, j], dst_ref=zbuf.at[phase, j],
            send_sem=zsend.at[phase, j], recv_sem=zrecv.at[phase, j],
            device_id=(j, c), device_id_type=MESH,
        )

    def triangle(phase, b, value):
        zbuf[phase, r] = value
        for d in reversed(range(1, R)):
            @pl.when(r - d >= 0)
            def _():
                row_send(phase, r - d).start()
        zacc[...] = dot_t(zbuf[phase, r], mbuf[b, r])
        for d in range(1, R):
            @pl.when(r + d < R)
            def _():
                row_recv(phase, r + d).wait_recv()
                zacc[...] += dot_t(zbuf[phase, r + d], mbuf[b, r + d])
        return zacc[...].astype(BF16)

    def sol_send(b, n):
        p = peers[n]
        return pltpu.make_async_remote_copy(
            src_ref=fbuf.at[b], dst_ref=out.at[b, me],
            send_sem=fsend.at[b, n], recv_sem=frecv.at[b, c],
            device_id=(r, p), device_id_type=MESH,
        )

    def sol_recv(b, n):
        p = peers[n]
        return pltpu.make_async_remote_copy(
            src_ref=fbuf.at[b], dst_ref=out.at[b, slot(p)],
            send_sem=fsend.at[b, n], recv_sem=frecv.at[b, p],
            device_id=(r, p), device_id_type=MESH,
        )

    def gather_start(b):
        for n in range(C - 1):
            sol_send(b, n).start()
        own_copy(b).start()

    def gather_end(b):
        own_copy(b).wait()
        for n in range(C - 1):
            sol_recv(b, n).wait_recv()
            sol_send(b, n).wait_send()

    def own_copy(b):
        return pltpu.make_async_copy(fbuf.at[b], out.at[b, me], lsem.at[b])

    next_sol = triangle(0, 1, residual(1).astype(BF16))

    zbuf[1, r] = next_sol
    for d in reversed(range(1, R)):
        @pl.when(r - d >= 0)
        def _():
            row_send(1, r - d).start()

        @pl.when(r + d < R)
        def _():
            row_send(1, r + d).start()
    fbuf[1] = next_sol
    gather_start(1)

    zacc[...] = residual(0)
    for j in reversed(range(R)):
        @pl.when(r != j)
        def _():
            row_recv(1, j).wait_recv()
        zacc[...] -= dot_t(zbuf[1, j], mbuf[2, j])

    first_sol = triangle(2, 0, zacc[...].astype(BF16))
    fbuf[0] = first_sol
    gather_start(0)

    gather_end(1)
    gather_end(0)
    for b in (1, 0):
        x_copy(b).wait_send()
        for n in range(H - 1):
            y_copy(b, n, c).wait_send()
    for phase in range(3):
        for d in range(1, R):
            @pl.when(r - d >= 0)
            def _():
                row_send(phase, r - d).wait_send()
            if phase == 1:
                @pl.when(r + d < R)
                def _():
                    row_send(phase, r + d).wait_send()


def fused_shards(R, C, factor_panel, solved_trail, right_sides, diag_inverse, coupling):
    _, m, k = factor_panel.shape
    frames = solved_trail.shape[1]
    fs = frames // C
    nk = 4
    kc = k // nk
    any_spec = pl.BlockSpec(memory_space=pl.ANY)
    DMA = pltpu.SemaphoreType.DMA
    out = pl.pallas_call(
        functools.partial(kernel, R, C, nk),
        out_shape=pltpu.VMEM((2, C, fs, m), BF16),
        in_specs=[any_spec] * 5,
        out_specs=any_spec,
        scratch_shapes=[
            pltpu.VMEM((2, nk, m, kc), BF16),
            pltpu.VMEM((nk, kc, frames), BF16),
            pltpu.VMEM((2, m, frames), BF16),
            pltpu.VMEM((3, R, m, m), BF16),
            pltpu.VMEM((m, frames), F32),
            pltpu.VMEM((2, C, fs, m), F32),
            pltpu.VMEM((2, C, fs, m), F32),
            pltpu.VMEM((2, C, fs, m), BF16),
            pltpu.VMEM((2, C, fs, m), BF16),
            pltpu.VMEM((3, R, fs, m), BF16),
            pltpu.VMEM((fs, m), F32),
            pltpu.VMEM((2, fs, m), BF16),
            pltpu.VMEM((2, C // 2, fs, m), BF16),
            pltpu.VMEM((2, C // 2, fs, m), BF16),
            DMA((2, nk)),
            DMA((nk,)),
            DMA,
            DMA((3, R)),
            DMA((2,)),
            DMA((2, C // 2)),
            DMA((2, C)),
            DMA((3, R)),
            DMA((3, R)),
            DMA((2, C - 1)),
            DMA((2, C)),
            DMA((2,)),
            DMA((2,)),
        ],
        compiler_params=pltpu.CompilerParams(collective_id=0, has_side_effects=True),
    )(factor_panel, solved_trail, right_sides, diag_inverse, coupling)
    return jnp.swapaxes(out.reshape(2, frames, m), 1, 2)


def solution(mesh):
    R, C = mesh.shape["row"], mesh.shape["col"]

    def shards(factor_panel, solved_trail, right_sides, diag_inverse, coupling):
        _, m, k = factor_panel.shape
        frames = solved_trail.shape[1]
        fits = (
            C > 2 and C & (C - 1) == 0 and frames % (16 * C) == 0 and m % 128 == 0
            and frames % 128 == 0 and k % 512 == 0
        )
        args = (factor_panel, solved_trail, right_sides, diag_inverse, coupling)
        return fused_shards(R, C, *args) if fits else plain_shards(*args)

    in_specs = (
        P(None, "row", "col"),
        P("col", None),
        P(None, "row", None),
        P(None, "row", None),
        P("row", None),
    )
    out_specs = P(None, "row", None)
    return jax.shard_map(shards, mesh=mesh, in_specs=in_specs, out_specs=out_specs, check_vma=False)
```

```python
import functools

import jax
import jax.numpy as jnp
from jax import lax
from jax.experimental import pallas as pl
from jax.experimental.pallas import tpu as pltpu
from jax.sharding import PartitionSpec as P

F32 = jnp.float32
BF16 = jnp.bfloat16
MESH = pl.DeviceIdType.MESH


def substitute(totals, rights, diag_inverse, coupling):
    next_res = (rights[1].astype(F32) - totals[1]).astype(BF16)
    next_all = lax.all_gather(next_res, "row", axis=0, tiled=True)
    next_sol = jnp.dot(diag_inverse[1], next_all, preferred_element_type=F32).astype(BF16)
    sol_all = lax.all_gather(next_sol, "row", axis=0, tiled=True)
    carried = jnp.dot(coupling, sol_all, preferred_element_type=F32)
    first_res = (rights[0].astype(F32) - totals[0] - carried).astype(BF16)
    first_all = lax.all_gather(first_res, "row", axis=0, tiled=True)
    first_sol = jnp.dot(diag_inverse[0], first_all, preferred_element_type=F32).astype(BF16)
    return jnp.stack([first_sol, next_sol])


def plain_shards(factor_panel, solved_trail, right_sides, diag_inverse, coupling):
    partial_value = jnp.einsum(
        "bik,kf->bif", factor_panel, solved_trail, preferred_element_type=F32
    )
    totals = lax.psum(partial_value, "col")
    return substitute(totals, right_sides, diag_inverse, coupling)


def dot_t(a, b):
    return lax.dot_general(a, b, (((1,), (1,)), ((), ())), preferred_element_type=F32)


def kernel(
    R, C, nk,
    panel, trail, right, diag, coup, out,
    pbuf, tbuf, hbuf, mbuf, acc, acc_t, h_t, sbuf, gbuf, zbuf, zacc, fbuf, xbuf, ybuf,
    psem, tsem, hsem, msem, lsem, gsend, grecv, zsend, zrecv, fsend, frecv, xsend, xrecv, vsend, vrecv,
):
    r = lax.axis_index("row")
    c = lax.axis_index("col")
    m, frames = hbuf.shape[1], hbuf.shape[2]
    kc = tbuf.shape[1]
    fs = frames // C

    def flip(d):
        total = 0
        bit = 1
        while bit < C:
            mine = (c // bit) % 2
            total = total + (((mine + 1) % 2) if d & bit else mine) * bit
            bit *= 2
        return total

    peers = [flip(d) for d in range(1, C)][::-1]
    H = C // 2
    def slot(p):
        return (p % 2) * H + p // 2
    core, mate = c % 2, flip(1)
    chips = [flip(d) for d in range(2, C, 2)][::-1]
    me = slot(c)

    def panel_copy(b, i):
        return pltpu.make_async_copy(
            panel.at[b, :, pl.ds(i * kc, kc)], pbuf.at[b, i], psem.at[b, i]
        )

    def trail_copy(i):
        return pltpu.make_async_copy(trail.at[pl.ds(i * kc, kc), :], tbuf.at[i], tsem.at[i])

    def mat_copy(b, j):
        src = coup.at[:, pl.ds(j * m, m)] if b == 2 else diag.at[b, :, pl.ds(j * m, m)]
        return pltpu.make_async_copy(src, mbuf.at[b, j], msem.at[b, j])

    right_copy = pltpu.make_async_copy(right, hbuf, hsem)
    for i in range(nk):
        trail_copy(i).start()
        panel_copy(1, i).start()
    def late0():
        for i in range(nk):
            panel_copy(0, i).start()
        right_copy.start()

    def late1():
        for b in (1, 2, 0):
            for j in range(R):
                mat_copy(b, j).start()


    barrier = pltpu.get_barrier_semaphore()
    for p in peers:
        pl.semaphore_signal(barrier, inc=1, device_id=(r, p), device_id_type=MESH)
    for d in range(1, R):
        pl.semaphore_signal(
            barrier, inc=1, device_id=(lax.rem(r + d, R), c), device_id_type=MESH
        )

    def partials(b):
        for i in range(nk):
            if b == 1:
                trail_copy(i).wait()
            panel_copy(b, i).wait()
            term = jnp.dot(pbuf[b, i], tbuf[i], preferred_element_type=F32)
            if i == 0:
                acc[...] = term
            else:
                acc[...] += term
        turned = acc[...].T.reshape(C, fs, m)
        sbuf[b] = turned.astype(BF16)
        acc_t[b] = turned


    def x_copy(b):
        return pltpu.make_async_remote_copy(
            src_ref=sbuf.at[b, pl.ds((1 - core) * H, H)], dst_ref=xbuf.at[b],
            send_sem=xsend.at[b], recv_sem=xrecv.at[b],
            device_id=(r, mate), device_id_type=MESH,
        )

    def y_copy(b, n, dst):
        p = chips[n]
        return pltpu.make_async_remote_copy(
            src_ref=ybuf.at[b, p // 2], dst_ref=gbuf.at[b, dst],
            send_sem=gsend.at[b, n], recv_sem=grecv.at[b, dst],
            device_id=(r, p), device_id_type=MESH,
        )

    def mid(b):
        x_copy(b).wait_recv()
        both = acc_t[b, pl.ds(core * H, H)] + xbuf[b].astype(F32)
        acc_t[b, pl.ds(core * H, H)] = both
        ybuf[b] = both.astype(BF16)
        for n in range(H - 1):
            y_copy(b, n, c).start()

    def first_send(b):
        x_copy(b).start()

    partials(1)
    late0()
    pl.semaphore_wait(barrier, C - 1 + R - 1)
    first_send(1)
    mid(1)
    partials(0)
    late1()
    first_send(0)
    right_copy.wait()
    h_t[1] = hbuf[1].astype(F32).T.reshape(C, fs, m)
    def residual(b):
        total = acc_t[b, me]
        for n in reversed(range(H - 1)):
            y_copy(b, n, chips[n]).wait_recv()
            total = total + gbuf[b, chips[n]].astype(F32)
        return h_t[b, me] - total

    def row_send(phase, j):
        return pltpu.make_async_remote_copy(
            src_ref=zbuf.at[phase, r], dst_ref=zbuf.at[phase, r],
            send_sem=zsend.at[phase, j], recv_sem=zrecv.at[phase, r],
            device_id=(j, c), device_id_type=MESH,
        )

    def row_recv(phase, j):
        return pltpu.make_async_remote_copy(
            src_ref=zbuf.at[phase, j], dst_ref=zbuf.at[phase, j],
            send_sem=zsend.at[phase, j], recv_sem=zrecv.at[phase, j],
            device_id=(j, c), device_id_type=MESH,
        )

    def triangle(phase, b, value):
        zbuf[phase, r] = value
        for d in reversed(range(1, R)):
            @pl.when(r - d >= 0)
            def _():
                row_send(phase, r - d).start()
        if phase == 0:
            mid(0)
            h_t[0] = hbuf[0].astype(F32).T.reshape(C, fs, m)
        for j in range(R):
            mat_copy(b, j).wait()
        zacc[...] = dot_t(zbuf[phase, r], mbuf[b, r])
        for d in range(1, R):
            @pl.when(r + d < R)
            def _():
                row_recv(phase, r + d).wait_recv()
                zacc[...] += dot_t(zbuf[phase, r + d], mbuf[b, r + d])
        return zacc[...].astype(BF16)

    def sol_send(b, n):
        p = peers[n]
        return pltpu.make_async_remote_copy(
            src_ref=fbuf.at[b], dst_ref=out.at[b, me],
            send_sem=fsend.at[b, n], recv_sem=frecv.at[b, c],
            device_id=(r, p), device_id_type=MESH,
        )

    def sol_recv(b, n):
        p = peers[n]
        return pltpu.make_async_remote_copy(
            src_ref=fbuf.at[b], dst_ref=out.at[b, slot(p)],
            send_sem=fsend.at[b, n], recv_sem=frecv.at[b, p],
            device_id=(r, p), device_id_type=MESH,
        )

    relayed = [0]
    skip = [chips[n] + 1 - 2 * core for n in relayed]
    def dnum(n):
        return C - 1 - n
    rel_d = [C - 2 - 2 * n for n in relayed]
    direct = [n for n in range(C - 1) if not (dnum(n) % 2 == 1 and dnum(n) - 1 in rel_d)]
    if relayed:
        direct = [n for n in direct if dnum(n) in rel_d] + [n for n in direct if dnum(n) not in rel_d]

    def relay(b, n, p):
        return pltpu.make_async_remote_copy(
            src_ref=out.at[b, slot(p)], dst_ref=out.at[b, slot(p)],
            send_sem=vsend.at[b, n], recv_sem=vrecv.at[b, n],
            device_id=(r, mate), device_id_type=MESH,
        )

    def gather_start(b):
        for n in direct:
            sol_send(b, n).start()
        own_copy(b).start()

    def gather_mid(b):
        for n in relayed:
            sol_recv(b, C - 1 - rel_d[n]).wait_recv()
            relay(b, n, chips[n]).start()

    def gather_end(b):
        own_copy(b).wait()
        for n in direct:
            if dnum(n) not in rel_d:
                sol_recv(b, n).wait_recv()
        for n in relayed:
            relay(b, n, flip(rel_d[n] + 1)).wait_recv()
        for n in direct:
            sol_send(b, n).wait_send()
        for n in relayed:
            relay(b, n, chips[n]).wait_send()

    def own_copy(b):
        return pltpu.make_async_copy(fbuf.at[b], out.at[b, me], lsem.at[b])

    next_sol = triangle(0, 1, residual(1).astype(BF16))

    zbuf[1, r] = next_sol
    for d in reversed(range(1, R)):
        @pl.when(r - d >= 0)
        def _():
            row_send(1, r - d).start()

        @pl.when(r + d < R)
        def _():
            row_send(1, r + d).start()
    fbuf[1] = next_sol
    gather_start(1)

    zacc[...] = residual(0)
    for j in range(R):
        mat_copy(2, j).wait()
    for j in reversed(range(R)):
        @pl.when(r != j)
        def _():
            row_recv(1, j).wait_recv()
        zacc[...] -= dot_t(zbuf[1, j], mbuf[2, j])

    gather_mid(1)
    first_sol = triangle(2, 0, zacc[...].astype(BF16))
    fbuf[0] = first_sol
    gather_start(0)

    gather_mid(0)
    gather_end(1)
    gather_end(0)
    for b in (1, 0):
        x_copy(b).wait_send()
        for n in range(H - 1):
            y_copy(b, n, c).wait_send()
    for phase in range(3):
        for d in range(1, R):
            @pl.when(r - d >= 0)
            def _():
                row_send(phase, r - d).wait_send()
            if phase == 1:
                @pl.when(r + d < R)
                def _():
                    row_send(phase, r + d).wait_send()


def fused_shards(R, C, factor_panel, solved_trail, right_sides, diag_inverse, coupling):
    _, m, k = factor_panel.shape
    frames = solved_trail.shape[1]
    fs = frames // C
    nk = 4
    kc = k // nk
    any_spec = pl.BlockSpec(memory_space=pl.ANY)
    DMA = pltpu.SemaphoreType.DMA
    out = pl.pallas_call(
        functools.partial(kernel, R, C, nk),
        out_shape=pltpu.VMEM((2, C, fs, m), BF16),
        in_specs=[any_spec] * 5,
        out_specs=any_spec,
        scratch_shapes=[
            pltpu.VMEM((2, nk, m, kc), BF16),
            pltpu.VMEM((nk, kc, frames), BF16),
            pltpu.VMEM((2, m, frames), BF16),
            pltpu.VMEM((3, R, m, m), BF16),
            pltpu.VMEM((m, frames), F32),
            pltpu.VMEM((2, C, fs, m), F32),
            pltpu.VMEM((2, C, fs, m), F32),
            pltpu.VMEM((2, C, fs, m), BF16),
            pltpu.VMEM((2, C, fs, m), BF16),
            pltpu.VMEM((3, R, fs, m), BF16),
            pltpu.VMEM((fs, m), F32),
            pltpu.VMEM((2, fs, m), BF16),
            pltpu.VMEM((2, C // 2, fs, m), BF16),
            pltpu.VMEM((2, C // 2, fs, m), BF16),
            DMA((2, nk)),
            DMA((nk,)),
            DMA,
            DMA((3, R)),
            DMA((2,)),
            DMA((2, C // 2)),
            DMA((2, C)),
            DMA((3, R)),
            DMA((3, R)),
            DMA((2, C - 1)),
            DMA((2, C)),
            DMA((2,)),
            DMA((2,)),
            DMA((2, C // 2)),
            DMA((2, C // 2)),
        ],
        compiler_params=pltpu.CompilerParams(collective_id=0, has_side_effects=True),
    )(factor_panel, solved_trail, right_sides, diag_inverse, coupling)
    return jnp.swapaxes(out.reshape(2, frames, m), 1, 2)


def solution(mesh):
    R, C = mesh.shape["row"], mesh.shape["col"]

    def shards(factor_panel, solved_trail, right_sides, diag_inverse, coupling):
        _, m, k = factor_panel.shape
        frames = solved_trail.shape[1]
        fits = (
            C > 2 and C & (C - 1) == 0 and frames % (16 * C) == 0 and m % 128 == 0
            and frames % 128 == 0 and k % 512 == 0
        )
        args = (factor_panel, solved_trail, right_sides, diag_inverse, coupling)
        return fused_shards(R, C, *args) if fits else plain_shards(*args)

    in_specs = (
        P(None, "row", "col"),
        P("col", None),
        P(None, "row", None),
        P(None, "row", None),
        P("row", None),
    )
    out_specs = P(None, "row", None)
    return jax.shard_map(shards, mesh=mesh, in_specs=in_specs, out_specs=out_specs, check_vma=False)
```
